32 devices in a mesh: groups: 2 (over x), seq: 16 (over z, y, core).
Axes of the slice: x: 2, y: 2, z: 4, core: 2. Of those that a mesh axis runs over, the one named last changes fastest.
Arguments:
- patches: bfloat16 [4096, 1176], P(('groups', 'seq')), parts along dimension 0, may hold values from -6 to 6
- row_owner: int32 [4096, 1], P(('groups', 'seq')), parts along dimension 0, may hold values from 0 to 15; in each aligned block of 128 rows (0 to 127, 128 to 255, ...) at most 16 rows name the same one
- window_slot: int32 [4096], P(('groups', 'seq')), parts along dimension 0, may hold values from 0 to 3
- w_patch: bfloat16 [1176, 1280], replicated, may hold values from -1 to 1
- vit_gain: float32 [1280], replicated, may hold values from 0.1 to 1.9
- w_qkv: bfloat16 [1280, 1920], replicated, may hold values from -1 to 1
- queries: bfloat16 [4096, 4096], P(('groups', 'seq')), parts along dimension 0, may hold values from -36 to 36
- new_kv: bfloat16 [4096, 1024], P(('groups', 'seq')), parts along dimension 0, may hold values from -6 to 6
- kv_cache: bfloat16 [2048, 16, 1024], P(('groups', 'seq')), parts along dimension 0, may hold values from -6 to 6
- block_table: int32 [32, 64], P(('groups', 'seq')), parts along dimension 0, may hold values from -1 to 1023, as said below
Outputs:
- vision_out: bfloat16 [4096, 640], P(('groups', 'seq')), parts along dimension 0
- attention_out: bfloat16 [4096, 4096], P(('groups', 'seq')), parts along dimension 0
The draws below stay inside these ranges and needn't reach their ends.
There are 2 independent parts, one for each index of `groups`. The reference program is written for one: setup_inputs(seed, part) draws one part's arguments, and reference() takes and returns one part's arrays. A program takes and returns all parts, laid end to end along the dimension named above; an argument that names none is the same for every part. Nothing has to cross between parts.
Inputs may be any that keep to these rules, and one draw needn't show every extreme that they name: `row_owner`: in the rows of one device, each owner is named by at most 16 rows. `block_table`: block b is stored on device b // 64. Each row lists 8 or more distinct blocks, then -1 entries; at most 8 of a row's blocks lie on one device.
All inputs are finite; a program needn't handle non-finite values.
Results may differ from the reference program's by a relative error of at most 0.0093.
Values may be sent and summed in bfloat16 or wider, within the bound.
A program may use at most 64 MiB of HBM per device.

```python
import math
import jax
import jax.numpy as jnp
import numpy as np
from jax import lax

SRC_ROWS = 128
ROWS = 2048
CAP = 16
PATCH = 1176
VIT = 1280
VHEADS = 8
VHD = 80
VQKV = 640
WSLOTS = 4
TOK_DEV = 128
TOKENS = 2048
QHEADS = 32
KVH = 4
HD = 128
BT = 16
BLK_DEV = 64
TMAX = 64
N_SEQ = 16


def table_law(key):
    table_key = jax.random.fold_in(key, 101)
    star_key, perm_key, offset_key, length_key, longest_key = jax.random.split(table_key, 5)
    per_owner = 2 * TMAX // N_SEQ
    star_owner = jax.random.randint(star_key, (), 0, N_SEQ)
    reader_keys = jax.random.split(perm_key, N_SEQ)
    rest_owner = jax.vmap(lambda sub_key: jax.random.permutation(sub_key, N_SEQ - 1))(reader_keys) + 1
    owner_order = jnp.concatenate([jnp.zeros((N_SEQ, 1), jnp.int32), rest_owner.astype(jnp.int32)], axis=1)
    owners_all = (star_owner + owner_order) % N_SEQ
    slot_index = jnp.arange(TMAX)
    owner_entry = owners_all[:, slot_index // per_owner]
    offsets = jax.random.randint(offset_key, (N_SEQ, N_SEQ), 0, BLK_DEV)
    local_index = (jnp.take_along_axis(offsets, owner_entry, axis=1) + slot_index[None, :] % per_owner) % BLK_DEV
    lengths = jax.random.randint(length_key, (N_SEQ,), per_owner, TMAX + 1)
    longest = jax.random.randint(longest_key, (), 0, N_SEQ)
    lengths = jnp.where(jnp.arange(N_SEQ) == longest, TMAX, lengths)
    entries = owner_entry * BLK_DEV + local_index
    return jnp.where(slot_index[None, :] < lengths[:, None], entries, -1).astype(jnp.int32)


def cache_law(key):
    cache_key = jax.random.fold_in(key, 202)
    array_shape = (N_SEQ * BLK_DEV, BT, 2 * KVH * HD)
    values = jnp.clip(jax.random.normal(cache_key, array_shape, jnp.float32), -6.0, 6.0)
    return values


def draw_block_table(key, part):
    return table_law(key)


def draw_kv_cache(key, part):
    return cache_law(key).astype(jnp.bfloat16)


def draw_queries(key, part):
    query_key = jax.random.fold_in(key, 303)
    array_shape = (N_SEQ * TOK_DEV, QHEADS * HD)
    values = jnp.clip(jax.random.normal(query_key, array_shape, jnp.float32), -6.0, 6.0)
    return values.astype(jnp.bfloat16)


def draw_patches(key, part):
    patch_key = jax.random.fold_in(key, 707)
    row_count = N_SEQ * SRC_ROWS
    array_shape = (row_count, PATCH)
    values = jnp.clip(jax.random.normal(patch_key, array_shape, jnp.float32), -6.0, 6.0)
    return values.astype(jnp.bfloat16)


def draw_w_patch(key, part):
    weight_key = jax.random.fold_in(key, 505)
    array_shape = (PATCH, VIT)
    values = jnp.clip(jax.random.normal(weight_key, array_shape, jnp.float32), -6.0, 6.0) * PATCH ** (-0.5)
    return values.astype(jnp.bfloat16)


def draw_w_qkv(key, part):
    weight_key = jax.random.fold_in(key, 606)
    inner_width = VHEADS * VHD
    array_shape = (VIT, 3 * inner_width)
    values = jnp.clip(jax.random.normal(weight_key, array_shape, jnp.float32), -6.0, 6.0) * VIT ** (-0.5)
    return values.astype(jnp.bfloat16)


def place_ends(values, stream_key, low, top_value):
    longest = values.shape.index(max(values.shape))
    spots = []
    for shift in (0, 1):
        where = [jax.random.randint(jax.random.fold_in(stream_key, axis), (), 0, length) for axis, length in enumerate(values.shape)]
        where[longest] = (where[longest] + shift) % values.shape[longest]
        spots.append(tuple(where))
    return values.at[spots[0]].set(low).at[spots[1]].set(top_value)


def steps_of(rng, dims, shards, low, top_value):
    def one(position, parts):
        draws = jax.random.uniform(jax.random.fold_in(jax.random.fold_in(rng, 6), position), (parts,), jnp.float32, low / len(shards), top_value / len(shards))
        return jnp.repeat(jnp.exp(draws), dims[position] // parts).reshape((-1,) + (1,) * (len(dims) - position - 1))

    loudness = one(*shards[0])
    for cut in shards[1:]:
        loudness = loudness * one(*cut)
    return loudness


def assign_block(rng, own, number, rows, amount, top, limit, slope):
    ranking = jax.random.permutation(rng, amount)
    crowded, usual = portions_of(amount, rows * top, limit, slope, True), portions_of(amount, rows * top, limit, slope, False)
    places = jnp.arange(amount)

    def named(sizes, rotation):
        used = int((sizes > 0).sum())
        fixed = max(1, used // 4)
        passed = fixed + (places - fixed + rotation * (used - fixed)) % max(1, amount - fixed)
        return jnp.zeros((amount,), jnp.int32).at[ranking[jnp.where(places < fixed, places, passed)]].set(jnp.asarray(sizes, jnp.int32))

    sizes = jnp.where(number % 4 == 0, named(crowded, number // 4), named(usual, number - number // 4 - 1))
    mixed = jax.random.permutation(jax.random.fold_in(own, 3), amount)
    giver, receiver = mixed[0:amount // 2 * 2:2], mixed[1:amount // 2 * 2:2]
    room = jnp.minimum(sizes[giver] - 1, limit - sizes[receiver]) // 2
    room = jnp.where((giver == ranking[0]) | (receiver == ranking[0]) | (sizes[receiver] == 0), 0, jnp.maximum(room, 0))
    passed = jax.random.randint(jax.random.fold_in(own, 4), (amount // 2,), 0, 1 << 20) % (room + 1)
    sizes = sizes.at[giver].add(-passed).at[receiver].add(passed)
    labels = jnp.searchsorted(jnp.cumsum(sizes), jnp.arange(rows * top), side="right").astype(jnp.int32)
    table = labels.reshape(top, rows).T
    table = table[jax.random.permutation(jax.random.fold_in(own, 1), rows)]
    rotation = jax.random.randint(jax.random.fold_in(own, 2), (rows, 1), 0, top)
    return jnp.take_along_axis(table, (jnp.arange(top)[None, :] + rotation) % top, axis=1)


def portions_of(count, total, reach, skew, full):
    portions = [(1 << 20) // math.isqrt(standing ** skew) + 1 for standing in range(1, count + 1)]
    largest = reach if full else min(reach, max(-(-total // count), total * portions[0] // sum(portions)))
    least = 1 if total - largest >= count - 1 else 0
    counts, surplus = [largest] + [least] * (count - 1), total - largest - least * (count - 1)
    while surplus > 0:
        movable = [i for i in range(1, count) if counts[i] < largest] or [i for i in range(1, count) if counts[i] < reach]
        whole, remaining = sum([portions[i] for i in movable]), surplus
        for i in movable:
            extra = min(reach - counts[i], max(1, remaining * portions[i] // whole), surplus)
            counts[i] = counts[i] + extra
            surplus = surplus - extra
    return np.array(counts)


def bell_draw(stream_key, shape, deviation, reach, cuts=(), kind=jnp.bfloat16):
    values = deviation * jax.random.normal(stream_key, shape, jnp.float32)
    if cuts:
        values = values * steps_of(stream_key, shape, cuts, -0.22, 0.18)
    return jnp.clip(values, -reach, reach).astype(kind)


def setup_inputs(seed: int = 0, part: int = 0) -> dict:
    keys = jax.random.split(jax.random.key(seed), 11)
    own_keys = jax.random.split(jax.random.fold_in(keys[10], part), 11)
    patches = draw_patches(jax.random.fold_in(jax.random.fold_in(keys[10], part), 71), part)
    row_owner_keys = jax.random.split(jax.random.fold_in(own_keys[1], 1), ROWS // SRC_ROWS)
    row_owner_turns = jax.random.permutation(jax.random.fold_in(own_keys[1], 3), ROWS // SRC_ROWS)
    row_owner = jax.vmap(lambda own, number: assign_block(jax.random.fold_in(own_keys[1], 2), own, number, SRC_ROWS, N_SEQ, 1, CAP, 2))(row_owner_keys, row_owner_turns).reshape((ROWS, 1))
    window_slot = place_ends(jax.random.randint(own_keys[2], (ROWS,), 0, WSLOTS), jax.random.fold_in(own_keys[2], 1), 0, WSLOTS - 1).astype(jnp.int32)
    w_patch = draw_w_patch(jax.random.fold_in(keys[10], 71), part)
    vit_gain = jnp.clip(1.0 + 0.18 * jax.random.normal(keys[4], (VIT,), jnp.float32), 0.1, 1.9)
    w_qkv = draw_w_qkv(jax.random.fold_in(keys[10], 71), part)
    queries = draw_queries(jax.random.fold_in(jax.random.fold_in(keys[10], part), 71), part)
    new_kv = bell_draw(own_keys[7], (TOKENS, 2 * KVH * HD), 1.0, 6.0, ((0, 16),))
    kv_cache = draw_kv_cache(jax.random.fold_in(jax.random.fold_in(keys[10], part), 71), part)
    block_table = draw_block_table(jax.random.fold_in(jax.random.fold_in(keys[10], part), 71), part)
    return dict(patches=patches, row_owner=row_owner, window_slot=window_slot, w_patch=w_patch, vit_gain=vit_gain, w_qkv=w_qkv, queries=queries, new_kv=new_kv, kv_cache=kv_cache, block_table=block_table)


def embed_rows(patch_rows, w_patch, vit_gain):
    embedded = jnp.dot(patch_rows, w_patch, preferred_element_type=jnp.float32).astype(jnp.bfloat16)
    widened = lax.optimization_barrier(embedded).astype(jnp.float32)
    factor = lax.rsqrt(lax.optimization_barrier(jnp.mean(widened * widened, axis=1, keepdims=True)) + 1e-06)
    return (widened * factor * vit_gain).astype(jnp.bfloat16)

def window_attention(qkv_rows, windows):
    total_rows = qkv_rows.shape[0]
    inner_width = VHEADS * VHD
    query_heads = qkv_rows[:, :inner_width].reshape(total_rows, VHEADS, VHD).astype(jnp.float32)
    key_heads = qkv_rows[:, inner_width:2 * inner_width].reshape(total_rows, VHEADS, VHD).astype(jnp.float32)
    value_heads = qkv_rows[:, 2 * inner_width:].reshape(total_rows, VHEADS, VHD).astype(jnp.float32)
    is_live = windows >= 0
    scores = jnp.einsum('qhd,khd->hqk', query_heads, key_heads) * VHD ** (-0.5)
    row_index = jnp.arange(total_rows)
    allowed = (windows[:, None] == windows[None, :]) & is_live[None, :] | (row_index[:, None] == row_index[None, :])
    scores = jnp.where(allowed[None], scores, -jnp.inf)
    highest = lax.optimization_barrier(jnp.max(scores, axis=2, keepdims=True))
    weights = jnp.exp(scores - highest)
    totals = lax.optimization_barrier(jnp.sum(weights, axis=2))
    rounded = lax.optimization_barrier(weights.astype(jnp.bfloat16)).astype(jnp.float32)
    blended = jnp.einsum('hqk,khd->qhd', rounded, value_heads)
    return (blended / totals.T[:, :, None]).reshape(total_rows, inner_width).astype(jnp.bfloat16)

def prompt_attention(query_rows, fresh_kv, cached_kv, cached_live):
    token_count = query_rows.shape[0]
    kv_width = KVH * HD
    group_size = QHEADS // KVH
    every_kv = jnp.concatenate([cached_kv, fresh_kv], axis=0).astype(jnp.float32)
    causal = jnp.arange(token_count)[None, :] <= jnp.arange(token_count)[:, None]
    allowed = jnp.concatenate([jnp.broadcast_to(cached_live[None, :], (token_count, cached_live.shape[0])), causal], axis=1)
    outputs = []
    for head_group in range(KVH):
        query_heads = query_rows[:, head_group * group_size * HD:(head_group + 1) * group_size * HD]
        query_heads = query_heads.reshape(token_count, group_size, HD).astype(jnp.float32)
        key_head = every_kv[:, head_group * HD:(head_group + 1) * HD]
        value_head = every_kv[:, kv_width + head_group * HD:kv_width + (head_group + 1) * HD]
        scores = jnp.einsum('cpd,kd->cpk', query_heads, key_head) * HD ** (-0.5)
        scores = jnp.where(allowed[:, None, :], scores, -jnp.inf)
        highest = lax.optimization_barrier(jnp.max(scores, axis=2, keepdims=True))
        weights = jnp.exp(scores - highest)
        totals = lax.optimization_barrier(jnp.sum(weights, axis=2))
        rounded = lax.optimization_barrier(weights.astype(jnp.bfloat16)).astype(jnp.float32)
        blended = jnp.einsum('cpk,kd->cpd', rounded, value_head)
        outputs.append((blended / totals[:, :, None]).reshape(token_count, group_size * HD))
    return jnp.concatenate(outputs, axis=1).astype(jnp.bfloat16)

def reference(patches, row_owner, window_slot, w_patch, vit_gain, w_qkv, queries, new_kv, kv_cache, block_table):
    normed = embed_rows(patches, w_patch, vit_gain)
    qkv_all = jnp.dot(normed, w_qkv, preferred_element_type=jnp.float32).astype(jnp.bfloat16)
    owner_ids = row_owner[:, 0]
    slot_count = 2 * SRC_ROWS

    def per_owner(owner):
        picked = jnp.nonzero(owner_ids == owner, size=slot_count, fill_value=ROWS)[0].astype(jnp.int32)
        is_live = picked < ROWS
        safe_rows = jnp.minimum(picked, ROWS - 1)
        windows = jnp.where(is_live, window_slot[safe_rows], -1)
        return (window_attention(qkv_all[safe_rows], windows), picked)
    attended, picked_rows = lax.map(per_owner, jnp.arange(N_SEQ, dtype=jnp.int32))
    vision_out = jnp.zeros((ROWS, VQKV), jnp.bfloat16).at[picked_rows.reshape(-1)].set(attended.reshape(-1, VQKV), mode='drop')

    def per_reader(reader):
        table_row = block_table[reader]
        is_live = table_row >= 0
        blocks = kv_cache[jnp.maximum(table_row, 0)]
        cached_kv = blocks.reshape(TMAX * BT, 2 * KVH * HD)
        cached_live = jnp.repeat(is_live, BT)
        first_row = (reader * TOK_DEV).astype(jnp.int32)
        query_rows = lax.dynamic_slice_in_dim(queries, first_row, TOK_DEV, 0)
        fresh_kv = lax.dynamic_slice_in_dim(new_kv, first_row, TOK_DEV, 0)
        return prompt_attention(query_rows, fresh_kv, cached_kv, cached_live)
    attention_out = lax.map(per_reader, jnp.arange(N_SEQ, dtype=jnp.int32)).reshape(TOKENS, QHEADS * HD)
    return (vision_out, attention_out)
```

```python
import functools

import jax
import jax.numpy as jnp
from jax import lax
from jax.experimental import pallas as pl
from jax.experimental.pallas import tpu as pltpu
from jax.sharding import PartitionSpec as P

VHEADS = 8
VHD = 80
QHEADS = 32
KVH = 4
HD = 128
DEAD = -1e30


def embed_rows(patch_rows, w_patch, vit_gain):
    embedded = jnp.dot(patch_rows, w_patch, preferred_element_type=jnp.float32).astype(jnp.bfloat16)
    widened = lax.optimization_barrier(embedded).astype(jnp.float32)
    factor = lax.rsqrt(jnp.mean(widened * widened, axis=1, keepdims=True) + 1e-06)
    return (widened * factor * vit_gain).astype(jnp.bfloat16)


def window_attention(qkv_rows, windows):
    total_rows = qkv_rows.shape[0]
    inner_width = VHEADS * VHD
    query_heads = qkv_rows[:, :inner_width].reshape(total_rows, VHEADS, VHD)
    key_heads = qkv_rows[:, inner_width : 2 * inner_width].reshape(total_rows, VHEADS, VHD)
    value_heads = qkv_rows[:, 2 * inner_width :].reshape(total_rows, VHEADS, VHD)
    is_live = windows >= 0
    every_row = jnp.arange(total_rows)
    scores = jnp.einsum(
        "qhd,khd->hqk", query_heads, key_heads, preferred_element_type=jnp.float32
    ) * VHD ** (-0.5)
    allowed = (windows[:, None] == windows[None, :]) & is_live[None, :] | (
        every_row[:, None] == every_row[None, :]
    )
    scores = jnp.where(allowed[None], scores, -jnp.inf)
    highest = jnp.max(scores, axis=2, keepdims=True)
    weights = jnp.exp(scores - highest)
    totals = jnp.sum(weights, axis=2)
    blended = jnp.einsum(
        "hqk,khd->qhd",
        weights.astype(jnp.bfloat16),
        value_heads,
        preferred_element_type=jnp.float32,
    )
    pieces = (blended / totals.T[:, :, None]).reshape(total_rows, inner_width)
    return pieces.astype(jnp.bfloat16)


def span_kernel(slots, q_ref, fresh_ref, bias_ref, kv_ref, o_ref, held, sems):
    tokens = q_ref.shape[0]
    table_len, block_tokens = held.shape[0] - tokens // kv_ref.shape[1], kv_ref.shape[1]
    group_size = QHEADS // KVH
    width = held.shape[2]

    def copy_of(t):
        return pltpu.make_async_copy(kv_ref.at[slots[t]], held.at[t], sems.at[t])

    fresh_copy = pltpu.make_async_copy(
        fresh_ref, held.at[pl.ds(table_len, tokens // block_tokens)], sems.at[table_len]
    )
    fresh_copy.start()
    for t in range(table_len):
        copy_of(t).start()
    for t in range(table_len):
        copy_of(t).wait()
    fresh_copy.wait()
    keys = held.shape[0] * block_tokens
    rows = 2 * tokens
    causal = lax.broadcasted_iota(jnp.int32, (rows, keys), 1) - table_len * block_tokens <= lax.rem(
        lax.broadcasted_iota(jnp.int32, (rows, keys), 0), tokens
    )
    bias = jnp.where(causal, bias_ref[...], DEAD)
    for g in range(KVH):
        key_head = held[:, :, g * HD : (g + 1) * HD].reshape(keys, HD)
        value_head = held[:, :, width // 2 + g * HD : width // 2 + (g + 1) * HD].reshape(keys, HD)
        for pair in range(group_size // 2):
            first = g * group_size + 2 * pair
            query = jnp.concatenate(
                [q_ref[:, (first + i) * HD : (first + i + 1) * HD] for i in range(2)], axis=0
            )
            scores = lax.dot_general(
                query, key_head, (((1,), (1,)), ((), ())), preferred_element_type=jnp.float32
            ) * HD ** (-0.5) + bias
            highest = jnp.max(scores, axis=1, keepdims=True)
            weights = jnp.exp(scores - highest)
            totals = jnp.sum(weights, axis=1, keepdims=True)
            blended = jnp.dot(
                weights.astype(jnp.bfloat16), value_head, preferred_element_type=jnp.float32
            )
            out = (blended / totals).astype(jnp.bfloat16)
            for i in range(2):
                o_ref[:, (first + i) * HD : (first + i + 1) * HD] = out[i * tokens : (i + 1) * tokens]


def prompt_attention(queries, new_kv, delivered, slots, table_live):
    tokens = queries.shape[0]
    table_len = slots.shape[0]
    block_tokens, width = delivered.shape[1:]
    held_blocks = table_len + tokens // block_tokens
    bias = jnp.concatenate(
        [
            jnp.where(jnp.repeat(table_live, block_tokens), 0.0, DEAD),
            jnp.zeros((tokens,), jnp.float32),
        ]
    ).astype(jnp.float32)[None, :]
    return pl.pallas_call(
        span_kernel,
        out_shape=jax.ShapeDtypeStruct(queries.shape, jnp.bfloat16),
        grid_spec=pltpu.PrefetchScalarGridSpec(
            num_scalar_prefetch=1,
            in_specs=[
                pl.BlockSpec(memory_space=pltpu.VMEM),
                pl.BlockSpec(memory_space=pl.ANY),
                pl.BlockSpec(memory_space=pltpu.VMEM),
                pl.BlockSpec(memory_space=pl.ANY),
            ],
            out_specs=pl.BlockSpec(memory_space=pltpu.VMEM),
            scratch_shapes=[
                pltpu.VMEM((held_blocks, block_tokens, width), jnp.bfloat16),
                pltpu.SemaphoreType.DMA((table_len + 1,)),
            ],
        ),
        compiler_params=pltpu.CompilerParams(vmem_limit_bytes=40 << 20),
        name="span",
    )(slots, queries, new_kv.reshape(tokens // block_tokens, block_tokens, width), bias, delivered)


def route_kernel(
    devices,
    capacity,
    scale_dims,
    patches_hbm,
    owner_ref,
    window_ref,
    w_patch_hbm,
    gain_ref,
    w_qkv_hbm,
    queries_hbm,
    fresh_hbm,
    cache_hbm,
    table_ref,
    vision_ref,
    span_ref,
    patches,
    w_patch,
    w_qkv,
    cache,
    query,
    fresh,
    tables,
    picks,
    picks_smem,
    staged,
    spans,
    span_bias,
    outgoing,
    arrived,
    qkv,
    attended,
    returned,
    top,
    total,
    blend,
    load_sems,
    query_sems,
    pick_sem,
    table_send,
    table_recv,
    row_send,
    row_recv,
    span_send,
    span_recv,
    back_send,
    back_recv,
):
    vit, blocks_dev, block_tokens = scale_dims
    me = lax.axis_index("seq")
    tokens = fresh.shape[0]
    per_owner = tables.shape[1]
    chunk = per_owner * block_tokens
    inner = VHEADS * VHD
    group_rows = QHEADS // KVH * tokens
    kv_width = KVH * HD

    def peer(k):
        other = me
        bit = 1
        while bit < devices:
            if (k // bit) % 2:
                other = other + bit * (1 - 2 * ((me // bit) % 2))
            bit *= 2
        return other

    def remote(src, dst, send, recv, k):
        return pltpu.make_async_remote_copy(
            src_ref=src,
            dst_ref=dst,
            send_sem=send.at[k],
            recv_sem=recv.at[k],
            device_id={"seq": peer(k)},
            device_id_type=pl.DeviceIdType.MESH,
        )

    def table_copy(k):
        return remote(tables.at[0], tables.at[k], table_send, table_recv, k)

    def row_copy(k):
        rows = pl.ds(k * capacity, capacity)
        return remote(outgoing.at[rows], arrived.at[rows], row_send, row_recv, k)

    def span_copy(k):
        rows = pl.ds(k * chunk, chunk)
        return remote(staged.at[rows], spans.at[rows], span_send, span_recv, k)

    def back_copy(k):
        rows = pl.ds(k * capacity, capacity)
        return remote(attended.at[rows], returned.at[rows], back_send, back_recv, k)

    others = range(1, devices)
    tables[0] = jnp.concatenate(
        [
            jnp.broadcast_to(table_ref[...], (per_owner, table_ref.shape[1])),
            jnp.full((per_owner, HD - table_ref.shape[1]), -1, jnp.int32),
        ],
        axis=1,
    )
    pairs = (
        (patches_hbm, patches),
        (w_patch_hbm, w_patch),
        (cache_hbm, cache),
        (w_qkv_hbm, w_qkv),
        (fresh_hbm, fresh),
    )
    loads = [pltpu.make_async_copy(a, b, load_sems.at[i]) for i, (a, b) in enumerate(pairs)]
    for load in loads:
        load.start()
    query_loads = [
        pltpu.make_async_copy(
            queries_hbm.at[:, pl.ds(h * HD, HD)],
            query.at[pl.ds(h * tokens, tokens)],
            query_sems.at[h],
        )
        for h in range(QHEADS)
    ]
    for load in query_loads:
        load.start()

    barrier = pltpu.get_barrier_semaphore()
    for k in others:
        pl.semaphore_signal(
            barrier, inc=1, device_id={"seq": peer(k)}, device_id_type=pl.DeviceIdType.MESH
        )
    src_rows = owner_ref.shape[1]
    patch = patches.shape[0]
    whole = patch // HD * HD
    rest = patch - whole
    flip = (((0,), (0,)), ((), ()))
    contract = (((1,), (1,)), ((), ()))
    sublanes = lax.broadcasted_iota(jnp.int32, (HD, src_rows), 0)
    route = jnp.bitwise_xor(owner_ref[...], me)
    route_hits = sublanes == route
    upper = lax.broadcasted_iota(jnp.int32, (src_rows, src_rows), 0) < lax.broadcasted_iota(
        jnp.int32, (src_rows, src_rows), 1
    )
    earlier = jnp.dot(
        jnp.where(route_hits, 1.0, 0.0).astype(jnp.bfloat16),
        jnp.where(upper, 1.0, 0.0).astype(jnp.bfloat16),
        preferred_element_type=jnp.float32,
    )
    ranks = jnp.sum(jnp.where(route_hits, earlier, 0.0), axis=0, keepdims=True).astype(jnp.int32)
    slot_count = outgoing.shape[0]
    slot_hits = jnp.where(
        lax.broadcasted_iota(jnp.int32, (slot_count, src_rows), 0) == route * capacity + ranks,
        1.0,
        0.0,
    ).astype(jnp.bfloat16)
    tags = jnp.where(
        lax.broadcasted_iota(jnp.int32, (HD - rest, src_rows), 0) == window_ref[...], 1.0, 0.0
    ).astype(jnp.bfloat16)
    loads[0].wait()
    outgoing[:, 0:whole] = lax.dot_general(
        slot_hits, patches[0:whole], (((1,), (1,)), ((), ())), preferred_element_type=jnp.float32
    ).astype(jnp.bfloat16)
    outgoing[:, whole:] = lax.dot_general(
        slot_hits,
        jnp.concatenate([patches[whole:patch], tags], axis=0),
        contract,
        preferred_element_type=jnp.float32,
    ).astype(jnp.bfloat16)
    arrived[0:capacity] = outgoing[0:capacity]
    pl.semaphore_wait(barrier, devices - 1)
    for k in others:
        table_copy(k).start()
    for k in reversed(others):
        row_copy(k).start()

    for k in others:
        table_copy(k).wait()
    asked = tables[...].reshape(devices * per_owner, HD)
    first = me * blocks_dev
    hits = (asked >= first) & (asked < first + blocks_dev)
    before = (
        lax.broadcasted_iota(jnp.int32, (HD, HD), 0) < lax.broadcasted_iota(jnp.int32, (HD, HD), 1)
    )
    places = jnp.dot(
        jnp.where(hits, 1.0, 0.0).astype(jnp.bfloat16),
        jnp.where(before, 1.0, 0.0).astype(jnp.bfloat16),
        preferred_element_type=jnp.float32,
    ).astype(jnp.int32)
    turn = lax.rem(lax.broadcasted_iota(jnp.int32, asked.shape, 0), per_owner)
    local = jnp.sum(
        jnp.where(hits & (places == turn), (asked - first).astype(jnp.float32), 0.0),
        axis=1,
        keepdims=True,
    ).astype(jnp.int32)
    picks[...] = jnp.broadcast_to(local, picks.shape)
    pick_copy = pltpu.make_async_copy(picks, picks_smem, pick_sem)
    pick_copy.start()
    loads[2].wait()
    pick_copy.wait()

    def gather(k):
        target = staged if k else spans
        for s in range(per_owner):
            pick = jnp.clip(picks_smem[k * per_owner + s, 0], 0, blocks_dev - 1)
            target[pl.ds(k * chunk + s * block_tokens, block_tokens), :] = cache[pick]
        if k:
            span_copy(k).start()

    far = devices // 2
    for k in [far, far + 1] + list(range(devices // 4, far)) + list(range(far + 2, devices)):
        gather(k)
    for k in range(devices // 4):
        gather(k)
    own = tables[0]
    step = lax.broadcasted_iota(jnp.int32, (per_owner, HD), 1)
    for k in range(devices):
        first = peer(k) * blocks_dev
        mine = (own >= first) & (own < first + blocks_dev)
        count = jnp.sum(jnp.where(mine, 1.0, 0.0), axis=1, keepdims=True).astype(jnp.int32)
        span_bias[k] = jnp.where(step < count * block_tokens, 0.0, DEAD)

    loads[4].wait()
    for load in query_loads:
        load.wait()
    causal = lax.rem(
        lax.broadcasted_iota(jnp.int32, (group_rows, tokens), 0), tokens
    ) >= lax.broadcasted_iota(jnp.int32, (group_rows, tokens), 1)
    for g in range(KVH):
        rows = slice(g * group_rows, (g + 1) * group_rows)
        scores = lax.dot_general(
            query[rows], fresh[:, g * HD : (g + 1) * HD], contract, preferred_element_type=jnp.float32
        ) * HD ** (-0.5)
        scores = jnp.where(causal, scores, DEAD)
        highest = jnp.max(scores, axis=1, keepdims=True)
        weights = jnp.exp(scores - highest)
        top[rows] = jnp.broadcast_to(highest, (group_rows, HD))
        total[rows] = weights
        blend[rows] = jnp.dot(
            weights.astype(jnp.bfloat16),
            fresh[:, kv_width + g * HD : kv_width + (g + 1) * HD],
            preferred_element_type=jnp.float32,
        )

    for k in others:
        row_copy(k).wait()
    loads[3].wait()
    loads[1].wait()
    embedded = (
        (
            jnp.dot(arrived[:, 0:whole], w_patch[0:whole], preferred_element_type=jnp.float32)
            + jnp.dot(
                arrived[:, whole:patch], w_patch[whole:patch], preferred_element_type=jnp.float32
            )
        )
        .astype(jnp.bfloat16)
        .astype(jnp.float32)
    )
    factor = lax.rsqrt(jnp.mean(embedded * embedded, axis=1, keepdims=True) + 1e-06)
    normed = (embedded * factor * gain_ref[...].reshape(1, vit)).astype(jnp.bfloat16)
    qkv[...] = jnp.dot(normed, w_qkv[...], preferred_element_type=jnp.float32).astype(jnp.bfloat16)
    marks = arrived[:, whole:]
    marks = jnp.where(
        lax.broadcasted_iota(jnp.int32, marks.shape, 1) >= rest, marks.astype(jnp.float32), 0.0
    ).astype(jnp.bfloat16)
    same = lax.dot_general(marks, marks, contract, preferred_element_type=jnp.float32)
    allowed = (same > 0.5) | (
        lax.broadcasted_iota(jnp.int32, same.shape, 0)
        == lax.broadcasted_iota(jnp.int32, same.shape, 1)
    )
    columns = lax.broadcasted_iota(jnp.int32, (slot_count, inner), 1)
    pieces = jnp.zeros((slot_count, inner), jnp.float32)
    for h in range(VHEADS):
        inside = (columns >= h * VHD) & (columns < (h + 1) * VHD)
        head_query = jnp.where(inside, qkv[:, 0:inner].astype(jnp.float32), 0.0).astype(jnp.bfloat16)
        scores = lax.dot_general(
            head_query, qkv[:, inner : 2 * inner], contract, preferred_element_type=jnp.float32
        ) * VHD ** (-0.5)
        scores = jnp.where(allowed, scores, DEAD)
        weights = jnp.exp(scores - jnp.max(scores, axis=1, keepdims=True))
        totals = jnp.sum(weights, axis=1, keepdims=True)
        blended = jnp.dot(
            weights.astype(jnp.bfloat16), qkv[:, 2 * inner :], preferred_element_type=jnp.float32
        )
        pieces = jnp.where(inside, blended / totals, pieces)
    attended[...] = pieces.astype(jnp.bfloat16)
    for k in others:
        back_copy(k).start()
    returned[0:capacity] = attended[0:capacity]

    def absorb(k, width, last=False):
        base = k * chunk
        bias = jnp.concatenate([span_bias[k + i, 0:1] for i in range(width)], axis=1)
        span = pl.ds(base, width * chunk)
        for g in range(KVH):
            rows = slice(g * group_rows, (g + 1) * group_rows)
            scores = lax.dot_general(
                query[rows],
                spans[span, g * HD : (g + 1) * HD],
                contract,
                preferred_element_type=jnp.float32,
            ) * HD ** (-0.5) + bias
            old = top[rows]
            highest = jnp.maximum(old, jnp.max(scores, axis=1, keepdims=True))
            shrink = jnp.exp(old - highest)
            parts = [
                jnp.exp(scores[:, i * chunk : (i + 1) * chunk] - highest) for i in range(width)
            ]
            summed = total[rows] * shrink
            for part in parts:
                summed = summed + part
            weights = jnp.concatenate([part.astype(jnp.bfloat16) for part in parts], axis=1)
            blended = blend[rows] * shrink + jnp.dot(
                weights,
                spans[span, kv_width + g * HD : kv_width + (g + 1) * HD],
                preferred_element_type=jnp.float32,
            )
            if last:
                out = (blended / jnp.sum(summed, axis=1, keepdims=True)).astype(jnp.bfloat16)
                for i in range(QHEADS // KVH):
                    h = g * (QHEADS // KVH) + i
                    span_ref[:, h * HD : (h + 1) * HD] = out[i * tokens : (i + 1) * tokens]
            else:
                top[rows] = highest
                total[rows] = summed
                blend[rows] = blended

    span_copy(1).wait()
    absorb(0, 2)
    for pair in range(1, devices // 2):
        span_copy(2 * pair).wait()
        span_copy(2 * pair + 1).wait()
        absorb(2 * pair, 2, pair == devices // 2 - 1)
    for k in others:
        back_copy(k).wait()
    vision_ref[...] = lax.dot_general(
        slot_hits, returned[...], flip, preferred_element_type=jnp.float32
    ).astype(jnp.bfloat16)


def routed(
    devices, capacity, patches, row_owner, window_slot, w_patch, vit_gain, w_qkv, queries, new_kv,
    kv_cache, block_table,
):
    src_rows, patch = patches.shape
    vit = w_patch.shape[1]
    inner = VHEADS * VHD
    tokens, width = new_kv.shape
    blocks_dev, block_tokens, _ = kv_cache.shape
    per_owner = 2 * block_table.shape[1] // devices
    slot_count = devices * capacity
    keys = devices * per_owner * block_tokens
    rows = QHEADS * tokens
    bf16, f32 = jnp.bfloat16, jnp.float32
    vmem, anywhere = pl.BlockSpec(memory_space=pltpu.VMEM), pl.BlockSpec(memory_space=pl.ANY)
    dma = pltpu.SemaphoreType.DMA
    return pl.pallas_call(
        functools.partial(route_kernel, devices, capacity, (vit, blocks_dev, block_tokens)),
        out_shape=(
            jax.ShapeDtypeStruct((src_rows, inner), bf16),
            jax.ShapeDtypeStruct(queries.shape, bf16),
        ),
        in_specs=[
            anywhere, vmem, vmem, anywhere, vmem, anywhere, anywhere, anywhere, anywhere, vmem,
        ],
        out_specs=(vmem, vmem),
        scratch_shapes=[
            pltpu.VMEM((patch, src_rows), bf16),
            pltpu.VMEM((patch, vit), bf16),
            pltpu.VMEM((vit, 3 * inner), bf16),
            pltpu.VMEM(kv_cache.shape, bf16),
            pltpu.VMEM((rows, HD), bf16),
            pltpu.VMEM((tokens, width), bf16),
            pltpu.VMEM((devices, per_owner, HD), jnp.int32),
            pltpu.VMEM((devices * per_owner, HD), jnp.int32),
            pltpu.SMEM((devices * per_owner, HD), jnp.int32),
            pltpu.VMEM((keys, width), bf16),
            pltpu.VMEM((keys, width), bf16),
            pltpu.VMEM((devices, per_owner, HD), f32),
            pltpu.VMEM((slot_count, patch // HD * HD + HD), bf16),
            pltpu.VMEM((slot_count, patch // HD * HD + HD), bf16),
            pltpu.VMEM((slot_count, 3 * inner), bf16),
            pltpu.VMEM((slot_count, inner), bf16),
            pltpu.VMEM((slot_count, inner), bf16),
            pltpu.VMEM((rows, HD), f32),
            pltpu.VMEM((rows, HD), f32),
            pltpu.VMEM((rows, HD), f32),
            dma((5,)),
            dma((QHEADS,)),
            dma,
        ]
        + [dma((devices,))] * 8,
        compiler_params=pltpu.CompilerParams(
            collective_id=0, has_side_effects=True, vmem_limit_bytes=56 << 20
        ),
        name="route",
    )(
        patches.T, row_owner.reshape(1, src_rows), window_slot.reshape(1, src_rows), w_patch,
        vit_gain, w_qkv, queries, new_kv, kv_cache, block_table,
    )


def shards(
    patches,
    row_owner,
    window_slot,
    w_patch,
    vit_gain,
    w_qkv,
    queries,
    new_kv,
    kv_cache,
    block_table,
):
    devices = lax.axis_size("seq")
    capacity = 2 * patches.shape[0] // devices
    per_owner = 2 * block_table.shape[1] // devices
    whole_tiles = capacity % 16 == 0 and per_owner == 8 and per_owner * kv_cache.shape[1] == HD
    if whole_tiles and devices & (devices - 1) == 0 and new_kv.shape[0] == HD and block_table.shape[1] < HD:
        return routed(
            devices, capacity, patches, row_owner, window_slot, w_patch, vit_gain, w_qkv, queries,
            new_kv, kv_cache, block_table,
        )
    table_row = block_table[0]
    table_len = table_row.shape[0]
    blocks_dev = kv_cache.shape[0]
    per_owner = max(1, 2 * table_len // devices)
    is_live = table_row >= 0
    holder = jnp.where(is_live, table_row // blocks_dev, -1)
    local_block = jnp.where(is_live, table_row % blocks_dev, 0)
    before_entry = jnp.arange(table_len)[:, None] > jnp.arange(table_len)[None, :]
    same_holder = (holder[:, None] == holder[None, :]) & is_live[None, :] & before_entry
    holder_rank = jnp.sum(same_holder.astype(jnp.int32), axis=1)
    request_slot = jnp.where(is_live, holder * per_owner + holder_rank, devices * per_owner)
    slot_hits = request_slot[:, None] == jnp.arange(devices * per_owner)[None, :]
    wanted = jnp.sum(jnp.where(slot_hits, local_block[:, None], 0), axis=0).astype(jnp.int32)
    asked = lax.all_to_all(
        wanted.reshape(devices, per_owner), "seq", split_axis=0, concat_axis=0, tiled=True
    )
    fetched = kv_cache[asked]
    delivered = lax.all_to_all(fetched, "seq", split_axis=0, concat_axis=0, tiled=True)

    src_rows = patches.shape[0]
    capacity = max(1, 2 * src_rows // devices)
    slot_count = devices * capacity
    owner_ids = row_owner[:, 0]
    owner_hits = (owner_ids[:, None] == jnp.arange(devices)[None, :]).astype(jnp.bfloat16)
    strictly_lower = (jnp.arange(src_rows)[:, None] > jnp.arange(src_rows)[None, :]).astype(
        jnp.bfloat16
    )
    earlier = jnp.dot(strictly_lower, owner_hits, preferred_element_type=jnp.float32)
    ranks = jnp.sum(earlier * owner_hits.astype(jnp.float32), axis=1).astype(jnp.int32)
    target_slot = owner_ids * capacity + ranks
    row_hits = jnp.arange(slot_count)[:, None] == target_slot[None, :]
    window_buffer = jnp.sum(jnp.where(row_hits, window_slot[None, :] + 1, 0), axis=1) - 1
    normed = embed_rows(patches, w_patch, vit_gain)
    outgoing = jnp.dot(
        row_hits.astype(jnp.bfloat16), normed, preferred_element_type=jnp.float32
    ).astype(jnp.bfloat16)
    tag = jnp.broadcast_to(window_buffer.astype(jnp.bfloat16)[:, None], (slot_count, HD))
    outgoing, fetched = lax.optimization_barrier(
        (jnp.concatenate([outgoing, tag], axis=1), fetched)
    )
    arrived = lax.all_to_all(
        outgoing.reshape(devices, capacity, -1), "seq", split_axis=0, concat_axis=0, tiled=True
    ).reshape(slot_count, -1)
    vit = normed.shape[1]
    arrived_windows = arrived[:, vit].astype(jnp.int32)
    qkv_rows = jnp.dot(arrived[:, :vit], w_qkv, preferred_element_type=jnp.float32).astype(
        jnp.bfloat16
    )
    attended = window_attention(qkv_rows, arrived_windows)
    returned = lax.all_to_all(
        attended.reshape(devices, capacity, -1), "seq", split_axis=0, concat_axis=0, tiled=True
    )
    vision_out = jnp.dot(
        row_hits.T.astype(jnp.bfloat16),
        returned.reshape(slot_count, -1),
        preferred_element_type=jnp.float32,
    ).astype(jnp.bfloat16)
    slots = jnp.where(is_live, request_slot, 0).astype(jnp.int32)
    attention_out = prompt_attention(
        queries,
        new_kv,
        delivered.reshape((devices * per_owner,) + kv_cache.shape[1:]),
        slots,
        is_live,
    )
    return (vision_out, attention_out)


def solution(mesh):
    in_specs = (
        P(("groups", "seq"), None),
        P(("groups", "seq"), None),
        P(("groups", "seq")),
        P(),
        P(),
        P(),
        P(("groups", "seq"), None),
        P(("groups", "seq"), None),
        P(("groups", "seq"), None, None),
        P(("groups", "seq"), None),
    )
    out_specs = (P(("groups", "seq"), None), P(("groups", "seq"), None))
    return jax.shard_map(shards, mesh=mesh, in_specs=in_specs, out_specs=out_specs, check_vma=False)
```
